32 devices in a mesh: groups: 2 (over x), sky: 16 (over z, y, core).
Axes of the slice: x: 2, y: 2, z: 4, core: 2. Of those that a mesh axis runs over, the one named last changes fastest.
Arguments:
- image: bfloat16 [32, 512, 128], P(('groups', 'sky')), parts along dimension 0, may hold values from -6 to 6
- row_taps: bfloat16 [40, 31], replicated, may hold values from -1 to 1
- col_taps: bfloat16 [40, 31], replicated, may hold values from -1 to 1
- mix_coeff: float32 [32, 3, 40], P(('groups', 'sky')), parts along dimension 0, may hold values from -1 to 1
- shift_frac: float32 [32, 2], P(('groups', 'sky')), parts along dimension 0, may hold values from 0.05 to 0.95
- ccd_visit: int32 [32], P(('groups', 'sky')), parts along dimension 0, may hold values from 0 to 3
- visit_weight: bfloat16 [8], P('groups'), parts along dimension 0, may hold values from 0.25 to 4
- tile_block: int32 [2048], P(('groups', 'sky')), parts along dimension 0, may hold values from 0 to 255, as said below
- tile_offset: int32 [2048], P(('groups', 'sky')), parts along dimension 0, may hold values from 0 to 7
Outputs:
- coadd: float32 [4096, 128], P(('groups', 'sky')), parts along dimension 0
- weight_map: float32 [4096], P(('groups', 'sky')), parts along dimension 0
The draws below stay inside these ranges and needn't reach their ends.
There are 2 independent parts, one for each index of `groups`. The reference program is written for one: setup_inputs(seed, part) draws one part's arguments, and reference() takes and returns one part's arrays. A program takes and returns all parts, laid end to end along the dimension named above; an argument that names none is the same for every part. Nothing has to cross between parts.
Inputs may be any that keep to these rules, and one draw needn't show every extreme that they name: `tile_block`: the owner of sky block b is device b // 16 of the sky axis. The 64 tiles of one window go to exactly 16 distinct owners, 4 tiles to each; at least four owners receive 4 tiles from every window.
All inputs are finite; a program needn't handle non-finite values.
Results may differ from the reference program's by a relative error of at most 0.0041.
Values may be sent and summed in bfloat16 or wider, within the bound.
A program may use at most 64 MiB of HBM per device.

```python
import math
import jax
import jax.numpy as jnp
from jax import lax

K = 40
TAPS = 31
VISITS = 4
TILE_R = 8
WC = 128
WR = 512
TILES_DEV = 64
CAP = 4
BLK_DEV = 16
SKY_HOLDERS = 16
CCDS = 16
TILES = 1024
SKY_ROWS = 2048


def draw_tile_block(key, part):
    keys = jax.random.split(jax.random.fold_in(key, 17), 5)
    dest_count = TILES_DEV // CAP
    demand_tally = jax.random.randint(keys[0], (SKY_HOLDERS,), 0, 2 ** 20)
    central_ranking = jax.random.permutation(keys[1], SKY_HOLDERS)
    central_reward = jnp.where(central_ranking < 4, 2 ** 22, 0)
    random_perturbation = jax.random.randint(keys[2], (SKY_HOLDERS, SKY_HOLDERS), 0, 2 ** 20)
    priority_values = (demand_tally[None, :] + central_reward[None, :] + random_perturbation) * SKY_HOLDERS + jnp.arange(SKY_HOLDERS)[None, :]
    priority_values = priority_values.astype(jnp.int32)
    unused_values, chosen = lax.top_k(priority_values, dest_count)
    shuffles = jax.vmap(lambda derived_random_key: jax.random.permutation(derived_random_key, TILES_DEV))(jax.random.split(keys[3], SKY_HOLDERS))
    owners = jnp.take_along_axis(chosen, shuffles // CAP, axis=1)
    local_block = jax.random.randint(keys[4], (SKY_HOLDERS, TILES_DEV), 0, BLK_DEV)
    return (owners * BLK_DEV + local_block).reshape(-1).astype(jnp.int32)


def plant(array, key, low, largest):
    extent = array.shape
    spot = [jax.random.randint(jax.random.fold_in(key, axis), (), 0, extent[axis]) for axis in range(len(extent))]
    array = array.at[tuple(spot)].set(low)
    longest = extent.index(max(extent))
    spot[longest] = (spot[longest] + 1) % extent[longest]
    return array.at[tuple(spot)].set(largest)


def steps_of(rng, dims, shards, smallest, largest):
    def one(position, blocks):
        steps = jax.random.uniform(jax.random.fold_in(jax.random.fold_in(rng, 6), position), (blocks,), jnp.float32, smallest / len(shards), largest / len(shards))
        return jnp.repeat(jnp.exp(steps), dims[position] // blocks).reshape((-1,) + (1,) * (len(dims) - position - 1))

    level = one(*shards[0])
    for cut in shards[1:]:
        level = level * one(*cut)
    return level


def bell_draw(rng, dims, deviation, reach, shards=(), held_as=jnp.bfloat16):
    values = jax.random.normal(rng, dims, jnp.float32) * deviation
    if len(shards) > 0:
        values = steps_of(rng, dims, shards, -0.22, 0.18) * values
    return jnp.clip(values, min=-reach, max=reach).astype(held_as)


def setup_inputs(seed: int = 0, part: int = 0) -> dict:
    streams_of = jax.random.split(jax.random.key(seed), 10)
    part_splits = jax.random.split(jax.random.fold_in(streams_of[9], part), 10)
    image = bell_draw(part_splits[0], (CCDS, WR, WC), 1.0, 6.0, ((0, 16),))
    row_taps = bell_draw(streams_of[1], (K, TAPS), TAPS ** -0.5, 1.0)
    col_taps = bell_draw(streams_of[2], (K, TAPS), TAPS ** -0.5, 1.0)
    mix_coeff = bell_draw(part_splits[3], (CCDS, 3, K), K ** -0.5, 1.0, ((0, 16),), jnp.float32)
    shift_frac = jnp.clip(0.05 + 0.9 * jax.random.uniform(part_splits[4], (CCDS, 2), jnp.float32) ** steps_of(part_splits[4], (CCDS, 2), ((0, 16),), -0.2, 0.2), 0.05, 0.95)
    ccd_visit = plant(jax.random.randint(part_splits[5], (CCDS,), 0, VISITS), jax.random.fold_in(part_splits[5], 1), 0, VISITS - 1).astype(jnp.int32)
    visit_weight = jnp.clip(jnp.exp(jax.random.uniform(part_splits[6], (VISITS,), jnp.float32, math.log(0.25), math.log(4.0))), 0.25, 4.0).astype(jnp.bfloat16)
    tile_block = draw_tile_block(jax.random.fold_in(jax.random.fold_in(streams_of[9], part), 71), part)
    tile_offset = plant(jax.random.randint(part_splits[8], (TILES,), 0, TILE_R), jax.random.fold_in(part_splits[8], 1), 0, TILE_R - 1).astype(jnp.int32)
    return {"image": image, "row_taps": row_taps, "col_taps": col_taps, "mix_coeff": mix_coeff, "shift_frac": shift_frac, "ccd_visit": ccd_visit, "visit_weight": visit_weight, "tile_block": tile_block, "tile_offset": tile_offset}


def lanczos_taps(fraction):
    positions = jnp.arange(-2, 4).astype(jnp.float32)
    offsets = positions[None, :] - fraction[:, None]
    angles = jnp.pi * offsets
    kernel = jnp.sin(angles) / angles * (jnp.sin(angles / 3.0) / (angles / 3.0))
    return kernel / jnp.sum(kernel, axis=1, keepdims=True)


def match_window(window, row_taps, col_taps, coefficients):
    half_taps = (TAPS - 1) // 2
    pixels = window.astype(jnp.float32)[None, None]
    kernel_row = row_taps.astype(jnp.float32)[:, None, None, :]
    smoothed = lax.conv_general_dilated(pixels, kernel_row, (1, 1), ((0, 0), (half_taps, half_taps)), dimension_numbers=("NCHW", "OIHW", "NCHW"), precision=lax.Precision.HIGHEST)
    smoothed = lax.optimization_barrier(smoothed.astype(jnp.bfloat16)).astype(jnp.float32)
    kernel_col = col_taps.astype(jnp.float32)[:, None, :, None]
    vertical = lax.conv_general_dilated(smoothed, kernel_col, (1, 1), ((half_taps, half_taps), (0, 0)), dimension_numbers=("NCHW", "OIHW", "NCHW"), feature_group_count=K, precision=lax.Precision.HIGHEST)[0]
    column_pos = (2.0 * jnp.arange(WC).astype(jnp.float32) + 1.0) / WC - 1.0
    row_pos = (2.0 * jnp.arange(WR).astype(jnp.float32) + 1.0) / WR - 1.0
    weights = coefficients[0][:, None, None] + coefficients[1][:, None, None] * column_pos[None, None, :] + coefficients[2][:, None, None] * row_pos[None, :, None]
    return jnp.sum(weights * vertical, axis=0)


def warp_window(matched, fraction):
    taps_across = lanczos_taps(fraction[1:2])[0]
    taps_down = lanczos_taps(fraction[0:1])[0]
    padded = jnp.pad(matched, ((0, 0), (2, 3)))
    spread = taps_across[0] * padded[:, 0:WC]
    for offset_index in range(1, 6):
        spread = spread + taps_across[offset_index] * padded[:, offset_index:offset_index + WC]
    padded = jnp.pad(spread, ((2, 3), (0, 0)))
    warped = taps_down[0] * padded[0:WR]
    for offset_index in range(1, 6):
        warped = warped + taps_down[offset_index] * padded[offset_index:offset_index + WR]
    return warped.astype(jnp.bfloat16)


def reference(image, row_taps, col_taps, mix_coeff, shift_frac, ccd_visit, visit_weight, tile_block, tile_offset):
    def one_window(packed):
        window, coefficients, fraction = packed
        return warp_window(match_window(window, row_taps, col_taps, coefficients), fraction)

    warped = lax.map(one_window, (image, mix_coeff, shift_frac))
    visit_match = ccd_visit[:, None] == jnp.arange(VISITS)[None, :]
    ccd_weight = jnp.sum(jnp.where(visit_match, visit_weight.astype(jnp.float32)[None, :], 0.0), axis=1)
    tile_weight = jnp.repeat(ccd_weight, TILES_DEV)
    tile_pixels = warped.reshape(CCDS * TILES_DEV, TILE_R, WC).astype(jnp.float32)
    weighted = tile_pixels * tile_weight[:, None, None]
    row_index = (tile_block[:, None] * TILE_R + tile_offset[:, None] + jnp.arange(TILE_R)[None, :]).astype(jnp.int32)
    sky_sum = jax.ops.segment_sum(weighted.reshape(-1, WC), row_index.reshape(-1), num_segments=SKY_ROWS + TILE_R)[:SKY_ROWS]
    row_weight = jnp.broadcast_to(tile_weight[:, None], (CCDS * TILES_DEV, TILE_R))
    weight_map = jax.ops.segment_sum(row_weight.reshape(-1), row_index.reshape(-1), num_segments=SKY_ROWS + TILE_R)[:SKY_ROWS]
    coadd = sky_sum / jnp.maximum(weight_map, 1.0)[:, None]
    return coadd, weight_map
```

```python
import functools

import jax
import jax.numpy as jnp
from jax import lax
from jax.experimental import pallas as pl
from jax.experimental.pallas import tpu as pltpu
from jax.sharding import PartitionSpec as P

TILE_R = 8
BLK_DEV = 16
LANES = 128
F32 = jnp.float32
BF16 = jnp.bfloat16


def iota(shape, axis):
    return lax.broadcasted_iota(jnp.int32, shape, axis)


def dot(lhs, rhs):
    return jnp.dot(lhs, rhs, preferred_element_type=F32)


def onehot(mask):
    return jnp.where(mask, 1.0, 0.0).astype(BF16)


def lanczos(fraction, rows):
    lane = iota((rows, LANES), 1)
    offsets = (lane - 2).astype(F32) - fraction
    offsets = jnp.where(lane < 6, offsets, 0.5)
    angles = jnp.pi * offsets
    thirds = angles / 3.0
    kernel = jnp.sin(angles) / angles * (jnp.sin(thirds) / thirds)
    kernel = jnp.where(lane < 6, kernel, 0.0)
    return kernel / jnp.sum(kernel, axis=1, keepdims=True)


def kernel(
    sky,
    image_ref,
    row_taps_ref,
    col_taps_ref,
    mix_ref,
    shift_ref,
    visit_ref,
    visit_weight_ref,
    block_ref,
    offset_ref,
    coadd_ref,
    weight_ref,
    xpad,
    lhs,
    rhs_hi,
    rhs_lo,
    taps2d,
    spread_pad,
    meta_send,
    meta_recv,
    data_send,
    data_recv,
    meta_ssem,
    meta_rsem,
    data_ssem,
    data_rsem,
):
    me = lax.axis_index("sky")
    win_rows, win_cols = image_ref.shape
    basis, tap_count = row_taps_ref.shape
    half = tap_count // 2
    tiles = block_ref.shape[1]
    cap = max(2, tiles // sky)
    span = cap * TILE_R
    owned_rows = BLK_DEV * TILE_R
    blk_shift = BLK_DEV.bit_length() - 1

    barrier = pltpu.get_barrier_semaphore()

    def greet(step, carry):
        pl.semaphore_signal(
            barrier,
            inc=1,
            device_id={"sky": lax.rem(me + step, sky)},
            device_id_type=pl.DeviceIdType.MESH,
        )
        return carry

    lax.fori_loop(1, sky, greet, 0)

    block = block_ref[...]
    owner_i = lax.shift_right_logical(block, blk_shift)
    start_row = ((block - owner_i * BLK_DEV) * TILE_R + offset_ref[...]).astype(F32)
    owner_row = owner_i.astype(F32)
    eye = iota((tiles, tiles), 0) == iota((tiles, tiles), 1)
    column = lambda row: jnp.sum(
        jnp.where(eye, jnp.broadcast_to(row, (tiles, tiles)), 0.0), axis=1, keepdims=True
    )
    owner_col = column(owner_row)
    start_col = column(start_row)
    same = owner_col == owner_row
    below = iota((tiles, tiles), 0) < iota((tiles, tiles), 1)
    above = iota((tiles, tiles), 1) < iota((tiles, tiles), 0)
    rank_row = jnp.sum(jnp.where(same & below, 1.0, 0.0), axis=0, keepdims=True)
    rank_col = jnp.sum(jnp.where(same & above, 1.0, 0.0), axis=1, keepdims=True)
    visits = visit_weight_ref.shape[1]
    own_weight = jnp.sum(
        jnp.where(
            iota((1, visits), 1) == visit_ref[0, 0], visit_weight_ref[...].astype(F32), 0.0
        ),
        axis=1,
        keepdims=True,
    )

    per_group = LANES // span
    sub = iota((sky * TILE_R, tiles), 0)
    to_owner = onehot(lax.shift_right_logical(sub, 3).astype(F32) == owner_row)
    lane = iota((tiles, LANES), 1)
    mine = lax.div(lane, jnp.int32(span)) == lax.rem(me, per_group)
    slot_rank = lax.div(lax.rem(lane, jnp.int32(span)), jnp.int32(TILE_R)).astype(F32)
    landing = start_col + (lax.rem(lane, jnp.int32(TILE_R)) + 1).astype(F32)
    landing = jnp.where(mine & (slot_rank == rank_col), landing, 0.0)
    targets = dot(to_owner, landing.astype(BF16))
    lane8 = iota((sky * TILE_R, LANES), 1)
    sub8 = lax.rem(iota((sky * TILE_R, LANES), 0), jnp.int32(TILE_R))
    weight8 = jnp.broadcast_to(own_weight, (sky * TILE_R, LANES))
    tile_lanes = lax.div(lane8, jnp.int32(span)) == lax.rem(me, per_group)
    spill_lanes = lax.div(lane8, jnp.int32(16)) == lax.rem(me, 8)
    header = jnp.where(
        sub8 == 0,
        targets,
        jnp.where(
            sub8 == 1,
            jnp.where(tile_lanes, weight8, 0.0),
            jnp.where((sub8 == 2) & spill_lanes, weight8, 0.0),
        ),
    )
    row_in = lax.rem(sub, jnp.int32(TILE_R)).astype(F32)
    before = lax.shift_right_logical(sub, 3).astype(F32) - 1.0
    over = onehot(
        (before == owner_row) & (start_row > row_in + float(owned_rows - TILE_R))
    )
    covered = dot(over, jnp.ones((tiles, LANES), BF16))
    meta_send[:, 0:TILE_R, :] = header.reshape(sky, TILE_R, LANES)
    meta_send[:, TILE_R:, :] = covered.reshape(sky, TILE_R, LANES)

    pl.semaphore_wait(barrier, sky - 1)

    def message(send, recv, ssem, rsem, step):
        to = lax.rem(me + step, sky)
        return pltpu.make_async_remote_copy(
            src_ref=send.at[to],
            dst_ref=recv.at[me],
            send_sem=ssem.at[step],
            recv_sem=rsem.at[step],
            device_id={"sky": to},
            device_id_type=pl.DeviceIdType.MESH,
        )

    def start_meta(step, carry):
        message(meta_send, meta_recv, meta_ssem, meta_rsem, step).start()
        return carry

    lax.fori_loop(1, sky, start_meta, 0)
    meta_recv[pl.ds(me, 1)] = meta_send[pl.ds(me, 1)]

    flip = onehot(
        iota((tap_count, LANES), 1)
        == lax.rem(half - iota((tap_count, LANES), 0) + LANES, jnp.int32(LANES))
    )
    rows_flipped = dot(row_taps_ref[...], flip)
    eye_k = onehot(iota((basis, basis), 0) == iota((basis, basis), 1))
    col_t = lax.dot_general(
        col_taps_ref[...], eye_k, (((0,), (0,)), ((), ())), preferred_element_type=F32
    )
    taps2d[...] = jnp.zeros_like(taps2d)
    for term in range(3):
        taps2d[term, 0:tap_count, :] = jnp.dot(
            col_t * mix_ref[term : term + 1, :],
            rows_flipped,
            preferred_element_type=F32,
            precision=lax.Precision.HIGHEST,
        )

    xpad[...] = jnp.zeros_like(xpad)
    xpad[pl.ds(16, win_rows), :] = image_ref[...].astype(F32)

    square = (win_cols, win_cols)
    band = jnp.abs(iota(square, 0) - iota(square, 1)) <= half
    column_pos = (2.0 * iota((1, win_cols), 1).astype(F32) + 1.0) / win_cols - 1.0

    def toeplitz(term, tap):
        row = jnp.broadcast_to(taps2d[term, pl.ds(tap, 1), :], square)
        return pltpu.roll(row, 0, 1, stride=1, stride_axis=0)

    def put(block_index, tap):
        here = pl.ds(block_index * win_cols, win_cols)
        both = (
            jnp.where(band, toeplitz(0, tap) + column_pos * toeplitz(1, tap), 0.0),
            jnp.where(band, toeplitz(2, tap), 0.0),
        )
        for side, value in enumerate(both):
            top = value.astype(BF16)
            rhs_hi[here, side * win_cols : (side + 1) * win_cols] = top
            rhs_lo[here, side * win_cols : (side + 1) * win_cols] = (
                value - top.astype(F32)
            ).astype(BF16)

    def build(tap, carry):
        put(2 * tap, tap)
        put(2 * tap + 1, tap + 16)
        return carry

    lax.fori_loop(0, 16, build, 0)
    for tap in range(16):
        moved = xpad[pl.ds(tap + 16 - half, win_rows + 16), :].astype(BF16)
        lhs[:, tap * 256 : tap * 256 + 128] = moved[0:win_rows]
        lhs[:, tap * 256 + 128 : tap * 256 + 256] = moved[16 : win_rows + 16]
    both = dot(lhs[...], rhs_hi[...]) + dot(lhs[...], rhs_lo[...])
    row_pos = (2.0 * iota((win_rows, win_cols), 0).astype(F32) + 1.0) / win_rows - 1.0
    matched = both[:, 0:win_cols] + row_pos * both[:, win_cols:]

    across = lanczos(shift_ref[0, 1], 8)
    down = lanczos(shift_ref[0, 0], 8)
    lanes = iota((win_rows, win_cols), 1)
    spread = across[0:1, 2:3] * matched
    for m in (-2, -1, 1, 2, 3):
        moved = pltpu.roll(matched, (-m) % win_cols, 1)
        keep = (lanes + m >= 0) & (lanes + m < win_cols)
        spread = spread + across[0:1, m + 2 : m + 3] * jnp.where(keep, moved, 0.0)
    spread_pad[0:8, :] = jnp.zeros((8, win_cols), F32)
    spread_pad[win_rows + 8 : win_rows + 16, :] = jnp.zeros((8, win_cols), F32)
    spread_pad[8 : win_rows + 8, :] = spread
    warped = down[0:1, 0:1] * spread_pad[pl.ds(6, win_rows), :]
    for m in range(-1, 4):
        warped = warped + down[0:1, m + 2 : m + 3] * spread_pad[pl.ds(8 + m, win_rows), :]
    warped = warped.astype(BF16)

    wide = tiles * TILE_R
    widen = onehot(
        iota((tiles, wide), 0) == lax.shift_right_logical(iota((tiles, wide), 1), 3)
    )
    in_tile = lax.rem(iota((1, wide), 1), jnp.int32(TILE_R)).astype(F32)
    spread8 = lambda row: dot(jnp.broadcast_to(row, (8, tiles)).astype(BF16), widen)[0:1, :]
    slot_lane = spread8(owner_row * cap + rank_row) * TILE_R + in_tile
    past = spread8(start_row) + in_tile - float(owned_rows)
    spill_lane = jnp.where(past >= 0.0, (spread8(owner_row) + 1.0) * TILE_R + past, -1.0)
    sent = sky * span
    pick = onehot(iota((sent, wide), 0).astype(F32) == slot_lane)
    data_send[:, 0:span, :] = dot(pick, warped).astype(BF16).reshape(sky, span, win_cols)
    pick = onehot(iota((sky * TILE_R, wide), 0).astype(F32) == spill_lane)
    spill = dot(pick, warped)
    spill_hi = spill.astype(BF16).astype(F32)
    spill_lo = spill - spill_hi
    data_send[:, span:, :] = jnp.concatenate(
        [spill_hi.reshape(sky, TILE_R, win_cols), spill_lo.reshape(sky, TILE_R, win_cols)],
        axis=1,
    ).astype(BF16)

    def start_data(step, carry):
        message(data_send, data_recv, data_ssem, data_rsem, step).start()
        return carry

    lax.fori_loop(1, sky, start_data, 0)
    data_recv[pl.ds(me, 1)] = data_send[pl.ds(me, 1)]

    def wait_meta(step, carry):
        copy = message(meta_send, meta_recv, meta_ssem, meta_rsem, step)
        copy.wait_send()
        copy.wait_recv()
        return carry

    lax.fori_loop(1, sky, wait_meta, 0)

    owned = (owned_rows, LANES)
    row_id = (iota(owned, 0) + 1).astype(F32)
    places = []
    total = jnp.zeros((owned_rows, win_cols), F32)
    ones = jnp.ones((LANES, win_cols), BF16)
    for group in range(sky // per_group):
        head = jnp.sum(
            meta_recv[group * per_group : (group + 1) * per_group, 0:TILE_R, :], axis=0
        )
        place = jnp.where(head[0:1, :] == row_id, head[1:2, :], 0.0).astype(BF16)
        places.append(place)
        total = total + dot(place, ones)
    spill_places = []
    same_row = lax.rem(iota(owned, 1), jnp.int32(TILE_R)) == iota(owned, 0)
    for group in range(sky // 8):
        head = jnp.sum(meta_recv[group * 8 : (group + 1) * 8, 0:TILE_R, :], axis=0)
        place = jnp.where(same_row, head[2:3, :], 0.0).astype(BF16)
        spill_places.append(place)
        count = meta_recv[group * 8 : (group + 1) * 8, TILE_R:, :]
        count = jnp.concatenate([count, jnp.zeros_like(count)], axis=1)
        total = total + dot(place, count.reshape(LANES, LANES).astype(BF16))
    diagonal = iota(owned, 0) == iota(owned, 1)
    weight_ref[...] = jnp.sum(jnp.where(diagonal, total, 0.0), axis=0, keepdims=True)

    def wait_data(step, carry):
        copy = message(data_send, data_recv, data_ssem, data_rsem, step)
        copy.wait_send()
        copy.wait_recv()
        return carry

    lax.fori_loop(1, sky, wait_data, 0)
    sums = jnp.zeros((owned_rows, win_cols), F32)
    for group, place in enumerate(places):
        part = data_recv[group * per_group : (group + 1) * per_group, 0:span, :]
        sums = sums + dot(place, part.reshape(LANES, win_cols))
    for group, place in enumerate(spill_places):
        part = data_recv[group * 8 : (group + 1) * 8, span:, :]
        sums = sums + dot(place, part.reshape(LANES, win_cols))
    coadd_ref[...] = sums / jnp.maximum(total, 1.0)


def on_device(
    image,
    row_taps,
    col_taps,
    mix_coeff,
    shift_frac,
    ccd_visit,
    visit_weight,
    tile_block,
    tile_offset,
):
    sky = lax.axis_size("sky")
    win_rows, win_cols = image.shape[1:]
    tiles = tile_block.shape[0]
    span = max(2, tiles // sky) * TILE_R
    owned_rows = BLK_DEV * TILE_R
    vmem = pl.BlockSpec(memory_space=pltpu.VMEM)
    smem = pl.BlockSpec(memory_space=pltpu.SMEM)
    coadd, weight_map = pl.pallas_call(
        functools.partial(kernel, sky),
        out_shape=(
            jax.ShapeDtypeStruct((owned_rows, win_cols), F32),
            jax.ShapeDtypeStruct((1, owned_rows), F32),
        ),
        in_specs=[vmem, vmem, vmem, vmem, smem, smem, vmem, vmem, vmem],
        out_specs=(vmem, vmem),
        scratch_shapes=[
            pltpu.VMEM((win_rows + 32, win_cols), F32),
            pltpu.VMEM((win_rows, 32 * win_cols), BF16),
            pltpu.VMEM((32 * win_cols, 2 * win_cols), BF16),
            pltpu.VMEM((32 * win_cols, 2 * win_cols), BF16),
            pltpu.VMEM((3, 32, LANES), F32),
            pltpu.VMEM((win_rows + 16, win_cols), F32),
            pltpu.VMEM((sky, 2 * TILE_R, LANES), F32),
            pltpu.VMEM((sky, 2 * TILE_R, LANES), F32),
            pltpu.VMEM((sky, span + 16, win_cols), BF16),
            pltpu.VMEM((sky, span + 16, win_cols), BF16),
            pltpu.SemaphoreType.DMA((sky,)),
            pltpu.SemaphoreType.DMA((sky,)),
            pltpu.SemaphoreType.DMA((sky,)),
            pltpu.SemaphoreType.DMA((sky,)),
        ],
        compiler_params=pltpu.CompilerParams(collective_id=0, has_side_effects=True),
        name="coadd",
    )(
        image[0],
        row_taps,
        col_taps,
        mix_coeff[0],
        shift_frac,
        ccd_visit.reshape(1, 1),
        visit_weight.reshape(1, -1),
        tile_block.reshape(1, -1),
        tile_offset.reshape(1, -1),
    )
    return coadd, weight_map.reshape(owned_rows)


def solution(mesh):
    return jax.shard_map(
        on_device,
        mesh=mesh,
        in_specs=(
            P(("groups", "sky"), None, None),
            P(),
            P(),
            P(("groups", "sky"), None, None),
            P(("groups", "sky"), None),
            P(("groups", "sky")),
            P("groups"),
            P(("groups", "sky")),
            P(("groups", "sky")),
        ),
        out_specs=(P(("groups", "sky"), None), P(("groups", "sky"))),
        check_vma=False,
    )
```

```python
import functools

import jax
import jax.numpy as jnp
from jax import lax
from jax.experimental import pallas as pl
from jax.experimental.pallas import tpu as pltpu
from jax.sharding import PartitionSpec as P

TILE_R = 8
BLK_DEV = 16
LANES = 128
STEPS = 4
F32 = jnp.float32
BF16 = jnp.bfloat16


def iota(shape, axis):
    return lax.broadcasted_iota(jnp.int32, shape, axis)


def dot(lhs, rhs):
    return jnp.dot(lhs, rhs, preferred_element_type=F32)


def onehot(mask):
    return jnp.where(mask, 1.0, 0.0).astype(BF16)


def lanczos(fraction):
    lane = iota((1, LANES), 1)
    offsets = (lane - 2).astype(F32) - fraction
    offsets = jnp.where(lane < 6, offsets, 0.5)
    angles = jnp.pi * offsets
    thirds = angles / 3.0
    kernel = jnp.sin(angles) / angles * (jnp.sin(thirds) / thirds)
    kernel = jnp.where(lane < 6, kernel, 0.0)
    return kernel / jnp.sum(kernel, axis=1, keepdims=True)


def kernel(
    sky,
    image_ref,
    row_taps_ref,
    col_taps_ref,
    mix_ref,
    shift_ref,
    visit_ref,
    visit_weight_ref,
    block_ref,
    offset_ref,
    result_ref,
    xpad,
    lhs,
    rhs,
    pick,
    taps2d,
    spread_pad,
    meta_send,
    meta_recv,
    data_send,
    data_recv,
    meta_ssem,
    meta_rsem,
    data_ssem,
    data_rsem,
):
    me = lax.axis_index("sky")
    win_rows, win_cols = image_ref.shape
    tap_count, basis = row_taps_ref.shape
    half = tap_count // 2
    tiles = block_ref.shape[1]
    cap = max(2, tiles // sky)
    span = cap * TILE_R
    owned_rows = BLK_DEV * TILE_R
    blk_shift = BLK_DEV.bit_length() - 1

    barrier = pltpu.get_barrier_semaphore()

    def greet(step, carry):
        pl.semaphore_signal(
            barrier,
            inc=1,
            device_id={"sky": lax.rem(me + step, sky)},
            device_id_type=pl.DeviceIdType.MESH,
        )
        return carry

    lax.fori_loop(1, sky, greet, 0)

    block = block_ref[...]
    owner_i = lax.shift_right_logical(block, blk_shift)
    start_row = ((block - owner_i * BLK_DEV) * TILE_R + offset_ref[...]).astype(F32)
    owner_row = owner_i.astype(F32)
    eye = iota((tiles, tiles), 0) == iota((tiles, tiles), 1)
    column = lambda row: jnp.sum(
        jnp.where(eye, jnp.broadcast_to(row, (tiles, tiles)), 0.0), axis=1, keepdims=True
    )
    owner_col = column(owner_row)
    start_col = column(start_row)
    same = owner_col == owner_row
    below = iota((tiles, tiles), 0) < iota((tiles, tiles), 1)
    above = iota((tiles, tiles), 1) < iota((tiles, tiles), 0)
    rank_row = jnp.sum(jnp.where(same & below, 1.0, 0.0), axis=0, keepdims=True)
    rank_col = jnp.sum(jnp.where(same & above, 1.0, 0.0), axis=1, keepdims=True)
    visits = visit_weight_ref.shape[1]
    own_weight = jnp.sum(
        jnp.where(
            iota((1, visits), 1) == visit_ref[...], visit_weight_ref[...].astype(F32), 0.0
        ),
        axis=1,
        keepdims=True,
    )

    per_group = LANES // span
    sub = iota((sky * TILE_R, tiles), 0)
    to_owner = onehot(lax.shift_right_logical(sub, 3).astype(F32) == owner_row)
    lane = iota((tiles, LANES), 1)
    mine = lax.div(lane, jnp.int32(span)) == lax.rem(me, per_group)
    slot_rank = lax.div(lax.rem(lane, jnp.int32(span)), jnp.int32(TILE_R)).astype(F32)
    landing = start_col + (lax.rem(lane, jnp.int32(TILE_R)) + 1).astype(F32)
    landing = jnp.where(mine & (slot_rank == rank_col), landing, 0.0)
    targets = dot(to_owner, landing.astype(BF16))
    lane8 = iota((sky * TILE_R, LANES), 1)
    sub8 = lax.rem(iota((sky * TILE_R, LANES), 0), jnp.int32(TILE_R))
    weight8 = jnp.broadcast_to(own_weight, (sky * TILE_R, LANES))
    tile_lanes = lax.div(lane8, jnp.int32(span)) == lax.rem(me, per_group)
    spill_lanes = lax.div(lane8, jnp.int32(16)) == lax.rem(me, 8)
    header = jnp.where(
        sub8 == 0,
        targets,
        jnp.where(
            sub8 == 1,
            jnp.where(tile_lanes, weight8, 0.0),
            jnp.where((sub8 == 2) & spill_lanes, weight8, 0.0),
        ),
    )
    row_in = lax.rem(sub, jnp.int32(TILE_R)).astype(F32)
    before = lax.shift_right_logical(sub, 3).astype(F32) - 1.0
    over = onehot(
        (before == owner_row) & (start_row > row_in + float(owned_rows - TILE_R))
    )
    covered = dot(over, jnp.ones((tiles, LANES), BF16))
    meta_send[:, 0:TILE_R, :] = header.reshape(sky, TILE_R, LANES)
    meta_send[:, TILE_R:, :] = covered.reshape(sky, TILE_R, LANES)

    pl.semaphore_wait(barrier, sky - 1)

    def message(send, recv, ssem, rsem, step):
        to = lax.rem(me + step, sky)
        return pltpu.make_async_remote_copy(
            src_ref=send.at[to],
            dst_ref=recv.at[me],
            send_sem=ssem,
            recv_sem=rsem,
            device_id={"sky": to},
            device_id_type=pl.DeviceIdType.MESH,
        )

    def wait_all(send, recv, ssem, rsem):
        copy = pltpu.make_async_remote_copy(
            src_ref=send.at[pl.ds(0, sky - 1)],
            dst_ref=recv.at[pl.ds(0, sky - 1)],
            send_sem=ssem,
            recv_sem=rsem,
            device_id={"sky": lax.rem(me + 1, sky)},
            device_id_type=pl.DeviceIdType.MESH,
        )
        copy.wait_send()
        copy.wait_recv()

    def start_meta(step, carry):
        message(meta_send, meta_recv, meta_ssem, meta_rsem, step).start()
        return carry

    lax.fori_loop(1, sky, start_meta, 0)
    meta_recv[pl.ds(me, 1)] = meta_send[pl.ds(me, 1)]

    flip = onehot(
        iota((tap_count, LANES), 1)
        == lax.rem(half - iota((tap_count, LANES), 0) + LANES, jnp.int32(LANES))
    )
    rows_flipped = lax.dot_general(
        row_taps_ref[...], flip, (((0,), (0,)), ((), ())), preferred_element_type=F32
    )
    col_t = col_taps_ref[...].astype(F32)
    taps2d[...] = jnp.zeros_like(taps2d)
    for term in range(3):
        taps2d[term, 0:tap_count, :] = jnp.dot(
            col_t * mix_ref[term],
            rows_flipped,
            preferred_element_type=F32,
            precision=lax.Precision.HIGHEST,
        )

    xpad[...] = jnp.zeros_like(xpad)
    xpad[pl.ds(16, win_rows), :] = image_ref[...].astype(F32)

    square = (win_cols, win_cols)
    band = jnp.abs(iota(square, 0) - iota(square, 1)) <= half
    column_pos = (2.0 * iota((1, win_cols), 1).astype(F32) + 1.0) / win_cols - 1.0

    def toeplitz(term, tap):
        row = jnp.broadcast_to(taps2d[term, pl.ds(tap, 1), :], square)
        return pltpu.roll(row, 0, 1, stride=1, stride_axis=0)

    def put(block_index, tap):
        here = pl.ds(block_index * win_cols, win_cols)
        both = (
            jnp.where(band, toeplitz(0, tap) + column_pos * toeplitz(1, tap), 0.0),
            jnp.where(band, toeplitz(2, tap), 0.0),
        )
        for side, value in enumerate(both):
            rhs[here, side * win_cols : (side + 1) * win_cols] = value.astype(BF16)

    wide = tiles * TILE_R
    widen = onehot(
        iota((tiles, wide), 0) == lax.shift_right_logical(iota((tiles, wide), 1), 3)
    )
    in_tile = lax.rem(iota((1, wide), 1), jnp.int32(TILE_R)).astype(F32)
    spread8 = lambda row: dot(jnp.broadcast_to(row, (8, tiles)).astype(BF16), widen)[0:1, :]
    slot_lane = spread8(owner_row * cap + rank_row) * TILE_R + in_tile
    past = spread8(start_row) + in_tile - float(owned_rows)
    spill_lane = jnp.where(past >= 0.0, (spread8(owner_row) + 1.0) * TILE_R + past, -1.0)
    sent = sky * span

    def build(first, last):
        for tap in range(first, last):
            put(2 * tap, tap)
            put(2 * tap + 1, tap + 16)
            moved = xpad[pl.ds(tap + 16 - half, win_rows + 16), :].astype(BF16)
            lhs[:, tap * 256 : tap * 256 + 128] = moved[0:win_rows]
            lhs[:, tap * 256 + 128 : tap * 256 + 256] = moved[16 : win_rows + 16]

    depth = 16 // STEPS
    both = None
    build(0, depth)
    for step in range(STEPS):
        if step + 1 < STEPS:
            build((step + 1) * depth, (step + 2) * depth)
        else:
            pick[0:sent, :] = onehot(iota((sent, wide), 0).astype(F32) == slot_lane)
            pick[sent:, :] = onehot(
                iota((sky * TILE_R, wide), 0).astype(F32) == spill_lane
            )
        inner = slice(step * depth * 256, (step + 1) * depth * 256)
        term = dot(lhs[:, inner], rhs[inner, :])
        both = term if both is None else both + term
    row_pos = (2.0 * iota((win_rows, win_cols), 0).astype(F32) + 1.0) / win_rows - 1.0
    matched = both[:, 0:win_cols] + row_pos * both[:, win_cols:]

    across = lanczos(shift_ref[0:1, 1:2])
    down = lanczos(shift_ref[0:1, 0:1])
    lanes = iota((win_rows, win_cols), 1)
    spread = across[0:1, 2:3] * matched
    for m in (-2, -1, 1, 2, 3):
        moved = pltpu.roll(matched, (-m) % win_cols, 1)
        keep = (lanes + m >= 0) & (lanes + m < win_cols)
        spread = spread + across[0:1, m + 2 : m + 3] * jnp.where(keep, moved, 0.0)
    spread_pad[0:8, :] = jnp.zeros((8, win_cols), F32)
    spread_pad[win_rows + 8 : win_rows + 16, :] = jnp.zeros((8, win_cols), F32)
    spread_pad[8 : win_rows + 8, :] = spread
    warped = down[0:1, 0:1] * spread_pad[pl.ds(6, win_rows), :]
    for m in range(-1, 4):
        warped = warped + down[0:1, m + 2 : m + 3] * spread_pad[pl.ds(8 + m, win_rows), :]
    warped = warped.astype(BF16)

    packed = dot(pick[...], warped)
    data_send[:, 0:span, :] = packed[0:sent].astype(BF16).reshape(sky, span, win_cols)
    spill = packed[sent:]
    spill_hi = spill.astype(BF16).astype(F32)
    spill_lo = spill - spill_hi
    data_send[:, span:, :] = jnp.concatenate(
        [spill_hi.reshape(sky, TILE_R, win_cols), spill_lo.reshape(sky, TILE_R, win_cols)],
        axis=1,
    ).astype(BF16)

    def start_data(step, carry):
        message(data_send, data_recv, data_ssem, data_rsem, step).start()
        return carry

    lax.fori_loop(1, sky, start_data, 0)
    data_recv[pl.ds(me, 1)] = data_send[pl.ds(me, 1)]

    wait_all(meta_send, meta_recv, meta_ssem, meta_rsem)

    owned = (owned_rows, LANES)
    row_id = (iota(owned, 0) + 1).astype(F32)
    places = []
    total = jnp.zeros((owned_rows, win_cols), F32)
    ones = jnp.ones((LANES, win_cols), BF16)
    for group in range(sky // per_group):
        head = jnp.sum(
            meta_recv[group * per_group : (group + 1) * per_group, 0:TILE_R, :], axis=0
        )
        place = jnp.where(head[0:1, :] == row_id, head[1:2, :], 0.0).astype(BF16)
        places.append(place)
        total = total + dot(place, ones)
    spill_places = []
    same_row = lax.rem(iota(owned, 1), jnp.int32(TILE_R)) == iota(owned, 0)
    for group in range(sky // 8):
        head = jnp.sum(meta_recv[group * 8 : (group + 1) * 8, 0:TILE_R, :], axis=0)
        place = jnp.where(same_row, head[2:3, :], 0.0).astype(BF16)
        spill_places.append(place)
        count = meta_recv[group * 8 : (group + 1) * 8, TILE_R:, :]
        count = jnp.concatenate([count, jnp.zeros_like(count)], axis=1)
        total = total + dot(place, count.reshape(LANES, LANES).astype(BF16))
    diagonal = iota(owned, 0) == iota(owned, 1)
    result_ref[owned_rows:, :] = jnp.broadcast_to(
        jnp.sum(jnp.where(diagonal, total, 0.0), axis=0, keepdims=True), (8, LANES)
    )

    wait_all(data_send, data_recv, data_ssem, data_rsem)
    sums = jnp.zeros((owned_rows, win_cols), F32)
    for group, place in enumerate(places):
        part = data_recv[group * per_group : (group + 1) * per_group, 0:span, :]
        sums = sums + dot(place, part.reshape(LANES, win_cols))
    for group, place in enumerate(spill_places):
        part = data_recv[group * 8 : (group + 1) * 8, span:, :]
        sums = sums + dot(place, part.reshape(LANES, win_cols))
    result_ref[0:owned_rows, :] = sums / jnp.maximum(total, 1.0)


def hand_over(result_ref, coadd_ref, weight_ref):
    owned_rows = coadd_ref.shape[0]
    coadd_ref[...] = result_ref[0:owned_rows, :]
    weight_ref[...] = result_ref[owned_rows : owned_rows + 1, :]


def on_device(
    image,
    row_taps,
    col_taps,
    mix_coeff,
    shift_frac,
    ccd_visit,
    visit_weight,
    tile_block,
    tile_offset,
):
    sky = lax.axis_size("sky")
    win_rows, win_cols = image.shape[1:]
    tiles = tile_block.shape[0]
    span = max(2, tiles // sky) * TILE_R
    owned_rows = BLK_DEV * TILE_R
    vmem = pl.BlockSpec(memory_space=pltpu.VMEM)
    result = pl.pallas_call(
        functools.partial(kernel, sky),
        out_shape=pltpu.VMEM((owned_rows + 8, win_cols), F32),
        in_specs=[vmem] * 9,
        out_specs=vmem,
        scratch_shapes=[
            pltpu.VMEM((win_rows + 32, win_cols), F32),
            pltpu.VMEM((win_rows, 32 * win_cols), BF16),
            pltpu.VMEM((32 * win_cols, 2 * win_cols), BF16),
            pltpu.VMEM((sky * (span + TILE_R), tiles * TILE_R), BF16),
            pltpu.VMEM((3, 32, LANES), F32),
            pltpu.VMEM((win_rows + 16, win_cols), F32),
            pltpu.VMEM((sky, 2 * TILE_R, LANES), F32),
            pltpu.VMEM((sky, 2 * TILE_R, LANES), F32),
            pltpu.VMEM((sky, span + 16, win_cols), BF16),
            pltpu.VMEM((sky, span + 16, win_cols), BF16),
            pltpu.SemaphoreType.DMA,
            pltpu.SemaphoreType.DMA,
            pltpu.SemaphoreType.DMA,
            pltpu.SemaphoreType.DMA,
        ],
        compiler_params=pltpu.CompilerParams(collective_id=0, has_side_effects=True),
        name="coadd",
    )(
        image[0],
        row_taps.T,
        col_taps.T,
        mix_coeff.transpose(1, 0, 2),
        shift_frac,
        ccd_visit.reshape(1, 1),
        visit_weight.reshape(1, -1),
        tile_block.reshape(1, -1),
        tile_offset.reshape(1, -1),
    )
    coadd, weight_map = pl.pallas_call(
        hand_over,
        out_shape=(
            jax.ShapeDtypeStruct((owned_rows, win_cols), F32),
            jax.ShapeDtypeStruct((1, owned_rows), F32),
        ),
        in_specs=[vmem],
        out_specs=(vmem, vmem),
        name="hand_over",
    )(pltpu.with_memory_space_constraint(result, pltpu.VMEM))
    return coadd, weight_map.reshape(owned_rows)


def solution(mesh):
    return jax.shard_map(
        on_device,
        mesh=mesh,
        in_specs=(
            P(("groups", "sky"), None, None),
            P(),
            P(),
            P(("groups", "sky"), None, None),
            P(("groups", "sky"), None),
            P(("groups", "sky")),
            P("groups"),
            P(("groups", "sky")),
            P(("groups", "sky")),
        ),
        out_specs=(P(("groups", "sky"), None), P(("groups", "sky"))),
        check_vma=False,
    )
```

```python
import functools

import jax
import jax.numpy as jnp
from jax import lax
from jax.experimental import pallas as pl
from jax.experimental.pallas import tpu as pltpu
from jax.sharding import PartitionSpec as P

TILE_R = 8
BLK_DEV = 16
LANES = 128
STEPS = 4
F32 = jnp.float32
BF16 = jnp.bfloat16


def iota(shape, axis):
    return lax.broadcasted_iota(jnp.int32, shape, axis)


def dot(lhs, rhs):
    return jnp.dot(lhs, rhs, preferred_element_type=F32)


def onehot(mask):
    return jnp.where(mask, 1.0, 0.0).astype(BF16)


def lanczos(fraction):
    lane = iota((1, LANES), 1)
    offsets = (lane - 2).astype(F32) - fraction
    offsets = jnp.where(lane < 6, offsets, 0.5)
    angles = jnp.pi * offsets
    thirds = angles / 3.0
    kernel = jnp.sin(angles) / angles * (jnp.sin(thirds) / thirds)
    kernel = jnp.where(lane < 6, kernel, 0.0)
    return kernel / jnp.sum(kernel, axis=1, keepdims=True)


def kernel(
    sky,
    image_ref,
    row_taps_ref,
    col_taps_ref,
    mix_ref,
    shift_ref,
    visit_ref,
    visit_weight_ref,
    block_ref,
    offset_ref,
    result_ref,
    xpad,
    lhs,
    rhs,
    pick,
    taps2d,
    acc,
    spread_pad,
    meta_send,
    meta_recv,
    data_send,
    data_recv,
    meta_ssem,
    meta_rsem,
    data_ssem,
    data_rsem,
):
    me = lax.axis_index("sky")
    win_rows, win_cols = image_ref.shape
    tap_count, basis = row_taps_ref.shape
    half = tap_count // 2
    tiles = block_ref.shape[1]
    cap = max(2, tiles // sky)
    span = cap * TILE_R
    owned_rows = BLK_DEV * TILE_R
    blk_shift = BLK_DEV.bit_length() - 1

    barrier = pltpu.get_barrier_semaphore()

    def greet(step, carry):
        pl.semaphore_signal(
            barrier,
            inc=1,
            device_id={"sky": lax.rem(me + step, sky)},
            device_id_type=pl.DeviceIdType.MESH,
        )
        return carry

    lax.fori_loop(1, sky, greet, 0)

    block = block_ref[...]
    owner_i = lax.shift_right_logical(block, blk_shift)
    start_row = ((block - owner_i * BLK_DEV) * TILE_R + offset_ref[...]).astype(F32)
    owner_row = owner_i.astype(F32)
    eye = iota((tiles, tiles), 0) == iota((tiles, tiles), 1)
    column = lambda row: jnp.sum(
        jnp.where(eye, jnp.broadcast_to(row, (tiles, tiles)), 0.0), axis=1, keepdims=True
    )
    owner_col = column(owner_row)
    start_col = column(start_row)
    same = owner_col == owner_row
    below = iota((tiles, tiles), 0) < iota((tiles, tiles), 1)
    above = iota((tiles, tiles), 1) < iota((tiles, tiles), 0)
    rank_row = jnp.sum(jnp.where(same & below, 1.0, 0.0), axis=0, keepdims=True)
    rank_col = jnp.sum(jnp.where(same & above, 1.0, 0.0), axis=1, keepdims=True)
    visits = visit_weight_ref.shape[1]
    own_weight = jnp.sum(
        jnp.where(
            iota((1, visits), 1) == visit_ref[...], visit_weight_ref[...].astype(F32), 0.0
        ),
        axis=1,
        keepdims=True,
    )

    per_group = LANES // span
    spill_group = min(LANES // TILE_R, sky)
    sub = iota((sky * TILE_R, tiles), 0)
    owner_of = lax.shift_right_logical(sub, 3).astype(F32)
    lane = iota((tiles, LANES), 1)
    mine = lax.div(lane, jnp.int32(span)) == lax.rem(me, per_group)
    slot_rank = lax.div(lax.rem(lane, jnp.int32(span)), jnp.int32(TILE_R)).astype(F32)
    in_eight = lax.rem(lane, jnp.int32(TILE_R)).astype(F32)
    landing = jnp.where(mine & (slot_rank == rank_col), start_col + in_eight + 1.0, 0.0)
    targets = dot(onehot(owner_of == owner_row), landing.astype(BF16))
    mine = lax.div(lane, jnp.int32(TILE_R)) == lax.rem(me, spill_group)
    cover = onehot(mine & (start_col > in_eight + float(owned_rows - TILE_R)))
    covered = dot(onehot(owner_of - 1.0 == owner_row), cover)
    lane8 = iota((sky * TILE_R, LANES), 1)
    sub8 = lax.rem(iota((sky * TILE_R, LANES), 0), jnp.int32(TILE_R))
    weight8 = jnp.broadcast_to(own_weight, (sky * TILE_R, LANES))
    tile_lanes = lax.div(lane8, jnp.int32(span)) == lax.rem(me, per_group)
    spill_lanes = lax.div(lane8, jnp.int32(TILE_R)) == lax.rem(me, spill_group)
    header = jnp.where((sub8 == 1) & tile_lanes, weight8, 0.0)
    header = jnp.where((sub8 == 2) & spill_lanes, weight8, header)
    header = jnp.where(sub8 == 3, covered * weight8, header)
    header = jnp.where(sub8 == 0, targets, header)
    meta_send[...] = header.reshape(sky, TILE_R, LANES)

    def message(send, recv, ssem, rsem, turn):
        away = lax.div(turn, 2)
        step = sky // 2 + jnp.where(lax.rem(turn, 2) == 1, away, -away)
        to = lax.rem(me + step, sky)
        return pltpu.make_async_remote_copy(
            src_ref=send.at[to],
            dst_ref=recv.at[me],
            send_sem=ssem,
            recv_sem=rsem,
            device_id={"sky": to},
            device_id_type=pl.DeviceIdType.MESH,
        )

    def wait_all(send, recv, ssem, rsem):
        copy = pltpu.make_async_remote_copy(
            src_ref=send.at[pl.ds(0, sky - 1)],
            dst_ref=recv.at[pl.ds(0, sky - 1)],
            send_sem=ssem,
            recv_sem=rsem,
            device_id={"sky": lax.rem(me + 1, sky)},
            device_id_type=pl.DeviceIdType.MESH,
        )
        copy.wait_send()
        copy.wait_recv()

    def start_meta(step, carry):
        message(meta_send, meta_recv, meta_ssem, meta_rsem, step).start()
        return carry

    def flip(place):
        tap = iota((tap_count, LANES), 0)
        return onehot(
            iota((tap_count, LANES), 1)
            == lax.rem(half + place - tap + LANES, jnp.int32(LANES))
        )

    def flipped(place):
        return lax.dot_general(
            row_taps_ref[...], flip(place), (((0,), (0,)), ((), ())), preferred_element_type=F32
        )

    def mixed(term, taps):
        return jnp.dot(
            col_taps_ref[...].astype(F32) * mix_ref[term],
            taps,
            preferred_element_type=F32,
            precision=lax.Precision.HIGHEST,
        )

    near, far = flipped(0), flipped(LANES // 2)
    taps2d[...] = jnp.zeros_like(taps2d)
    taps2d[0, 0:tap_count, :] = mixed(0, near) + mixed(2, far)
    taps2d[1, 0:tap_count, :] = mixed(1, near)

    xpad[...] = jnp.zeros_like(xpad)
    xpad[pl.ds(16, win_rows), :] = image_ref[...].astype(F32)

    square = (win_cols, win_cols)
    wrapped = lax.rem(iota(square, 1) + LANES // 2, jnp.int32(LANES))
    band = jnp.abs(iota(square, 0) - iota(square, 1)) <= half
    far_band = jnp.abs(iota(square, 0) - wrapped) <= half
    eight = (TILE_R, LANES)
    signed = lax.rem(iota(eight, 1) + LANES // 2, jnp.int32(LANES)) - LANES // 2
    column_pos = (2.0 * signed.astype(F32) + 1.0) / win_cols - 1.0

    def put(block_index, tap):
        here = pl.ds(block_index * win_cols, win_cols)
        fixed, slope = (
            pltpu.roll(
                jnp.broadcast_to(taps2d[term, tap : tap + 1, :], eight),
                0,
                1,
                stride=1,
                stride_axis=0,
            )
            for term in range(2)
        )
        fixed = fixed + column_pos * slope
        rows = []
        for first in range(0, win_cols, TILE_R):
            value = fixed + (2.0 * first / win_cols) * slope
            rows.append(pltpu.roll(value, first, 1) if first else value)
        value = jnp.concatenate(rows, axis=0)
        rhs[here, 0:win_cols] = jnp.where(band, value, 0.0).astype(BF16)
        rhs[here, win_cols:] = jnp.where(far_band, value, 0.0).astype(BF16)

    wide = tiles * TILE_R
    widen = onehot(
        iota((tiles, wide), 0) == lax.shift_right_logical(iota((tiles, wide), 1), 3)
    )
    in_tile = lax.rem(iota((1, wide), 1), jnp.int32(TILE_R)).astype(F32)
    spread8 = lambda row: dot(jnp.broadcast_to(row, (8, tiles)).astype(BF16), widen)[0:1, :]
    slot_lane = spread8(owner_row * cap + rank_row) * TILE_R + in_tile
    past = spread8(start_row) + in_tile - float(owned_rows)
    spill_lane = jnp.where(past >= 0.0, (spread8(owner_row) + 1.0) * TILE_R + past, -1.0)
    sent = sky * span

    def build(first, last):
        for tap in range(first, last):
            put(2 * tap, tap)
            put(2 * tap + 1, tap + 16)
            moved = xpad[pl.ds(tap + 16 - half, win_rows + 16), :].astype(BF16)
            lhs[:, tap * 256 : tap * 256 + 128] = moved[0:win_rows]
            lhs[:, tap * 256 + 128 : tap * 256 + 256] = moved[16 : win_rows + 16]

    depth = 16 // STEPS
    build(0, depth)
    for step in range(STEPS):
        if step + 1 < STEPS:
            build((step + 1) * depth, (step + 2) * depth)
        else:
            pick[0:sent, :] = onehot(iota((sent, wide), 0).astype(F32) == slot_lane)
            pick[sent:, :] = onehot(
                iota((sky * TILE_R, wide), 0).astype(F32) == spill_lane
            )
        inner = slice(step * depth * 256, (step + 1) * depth * 256)
        term = dot(lhs[:, inner], rhs[inner, :])
        acc[...] = term if step == 0 else acc[...] + term

    pl.semaphore_wait(barrier, sky - 1)
    lax.fori_loop(1, sky, start_meta, 0)
    meta_recv[pl.ds(me, 1)] = meta_send[pl.ds(me, 1)]

    across = lanczos(shift_ref[0:1, 1:2])
    down = lanczos(shift_ref[0:1, 0:1])
    lane = iota((1, win_cols), 1)
    chunk = min(64, win_rows)
    spread_pad[0:8, :] = jnp.zeros((8, win_cols), F32)
    spread_pad[win_rows + 8 : win_rows + 16, :] = jnp.zeros((8, win_cols), F32)
    across_taps = [
        jnp.where((lane + m >= 0) & (lane + m < win_cols), across[0:1, m + 2 : m + 3], 0.0)
        for m in range(-2, 4)
    ]
    down_taps = [
        jnp.broadcast_to(down[0:1, m + 2 : m + 3], (1, win_cols)) for m in range(-2, 4)
    ]
    for first in range(0, win_rows, chunk):
        here = slice(first, first + chunk)
        row_pos = (iota((chunk, win_cols), 0) + first).astype(F32)
        row_pos = (2.0 * row_pos + 1.0) / win_rows - 1.0
        sloped = pltpu.roll(acc[here, win_cols:], LANES // 2, 1)
        matched = acc[here, 0:win_cols] + row_pos * sloped
        spread = across_taps[2] * matched
        for m in (-2, -1, 1, 2, 3):
            spread = spread + across_taps[m + 2] * pltpu.roll(matched, (-m) % win_cols, 1)
        spread_pad[first + 8 : first + 8 + chunk, :] = spread
    warped = []
    for first in range(0, win_rows, chunk):
        value = down_taps[0] * spread_pad[pl.ds(first + 6, chunk), :]
        for m in range(-1, 4):
            value = value + down_taps[m + 2] * spread_pad[pl.ds(first + 8 + m, chunk), :]
        warped.append(value.astype(BF16))
    warped = jnp.concatenate(warped, axis=0)

    packed = dot(pick[...], warped)
    data_send[:, 0:span, :] = packed[0:sent].astype(BF16).reshape(sky, span, win_cols)
    data_send[:, span:, :] = packed[sent:].reshape(sky, TILE_R, win_cols).astype(BF16)

    def start_data(step, carry):
        message(data_send, data_recv, data_ssem, data_rsem, step).start()
        return carry

    lax.fori_loop(1, sky, start_data, 0)
    data_recv[pl.ds(me, 1)] = data_send[pl.ds(me, 1)]

    wait_all(meta_send, meta_recv, meta_ssem, meta_rsem)

    owned = (owned_rows, LANES)
    row_id = (iota(owned, 0) + 1).astype(F32)
    places = []
    total = jnp.zeros((owned_rows, win_cols), F32)
    ones = jnp.ones((LANES, win_cols), BF16)
    for group in range(sky // per_group):
        head = jnp.sum(
            meta_recv[group * per_group : (group + 1) * per_group], axis=0
        )
        place = jnp.where(head[0:1, :] == row_id, head[1:2, :], 0.0).astype(BF16)
        places.append(place)
        total = total + dot(place, ones)
    spill_places = []
    same_row = lax.rem(iota(owned, 1), jnp.int32(TILE_R)) == iota(owned, 0)
    here_row = lax.rem(iota(eight, 1), jnp.int32(TILE_R)) == iota(eight, 0)
    first_rows = jnp.zeros(eight, F32)
    for group in range(sky // spill_group):
        head = jnp.sum(meta_recv[group * spill_group : (group + 1) * spill_group], axis=0)
        spill_places.append(jnp.where(same_row, head[2:3, :], 0.0).astype(BF16))
        count = jnp.sum(jnp.where(here_row, head[3:4, :], 0.0), axis=1, keepdims=True)
        first_rows = first_rows + jnp.broadcast_to(count, eight)
    total = total + jnp.concatenate(
        [first_rows, jnp.zeros((owned_rows - TILE_R, LANES), F32)], axis=0
    )
    diagonal = iota(owned, 0) == iota(owned, 1)
    result_ref[owned_rows:, :] = jnp.broadcast_to(
        jnp.sum(jnp.where(diagonal, total, 0.0), axis=0, keepdims=True), (8, LANES)
    )

    wait_all(data_send, data_recv, data_ssem, data_rsem)
    sums = jnp.zeros((owned_rows, win_cols), F32)
    for group, place in enumerate(places):
        part = data_recv[group * per_group : (group + 1) * per_group, 0:span, :]
        sums = sums + dot(place, part.reshape(LANES, win_cols))
    for group, place in enumerate(spill_places):
        part = data_recv[group * spill_group : (group + 1) * spill_group, span:, :]
        part = part.astype(F32).reshape(spill_group * TILE_R, win_cols).astype(BF16)
        sums = sums + dot(place[:, 0 : spill_group * TILE_R], part)
    result_ref[0:owned_rows, :] = sums / jnp.maximum(total, 1.0)


def hand_over(result_ref, coadd_ref, weight_ref):
    owned_rows = coadd_ref.shape[0]
    coadd_ref[...] = result_ref[0:owned_rows, :]
    weight_ref[...] = result_ref[owned_rows : owned_rows + 1, :]


def on_device(
    image,
    row_taps,
    col_taps,
    mix_coeff,
    shift_frac,
    ccd_visit,
    visit_weight,
    tile_block,
    tile_offset,
):
    sky = lax.axis_size("sky")
    win_rows, win_cols = image.shape[1:]
    tiles = tile_block.shape[0]
    span = max(2, tiles // sky) * TILE_R
    owned_rows = BLK_DEV * TILE_R
    vmem = pl.BlockSpec(memory_space=pltpu.VMEM)
    result = pl.pallas_call(
        functools.partial(kernel, sky),
        out_shape=pltpu.VMEM((owned_rows + 8, win_cols), F32),
        in_specs=[vmem] * 9,
        out_specs=vmem,
        scratch_shapes=[
            pltpu.VMEM((win_rows + 32, win_cols), F32),
            pltpu.VMEM((win_rows, 32 * win_cols), BF16),
            pltpu.VMEM((32 * win_cols, 2 * win_cols), BF16),
            pltpu.VMEM((sky * (span + TILE_R), tiles * TILE_R), BF16),
            pltpu.VMEM((2, 32, LANES), F32),
            pltpu.VMEM((win_rows, 2 * win_cols), F32),
            pltpu.VMEM((win_rows + 16, win_cols), F32),
            pltpu.VMEM((sky, TILE_R, LANES), F32),
            pltpu.VMEM((sky, TILE_R, LANES), F32),
            pltpu.VMEM((sky, span + TILE_R, win_cols), BF16),
            pltpu.VMEM((sky, span + TILE_R, win_cols), BF16),
            pltpu.SemaphoreType.DMA,
            pltpu.SemaphoreType.DMA,
            pltpu.SemaphoreType.DMA,
            pltpu.SemaphoreType.DMA,
        ],
        compiler_params=pltpu.CompilerParams(collective_id=0, has_side_effects=True),
        name="coadd",
    )(
        image[0],
        row_taps.T,
        col_taps.T,
        mix_coeff.transpose(1, 0, 2),
        shift_frac,
        ccd_visit.reshape(1, 1),
        visit_weight.reshape(1, -1),
        tile_block.reshape(1, -1),
        tile_offset.reshape(1, -1),
    )
    coadd, weight_map = pl.pallas_call(
        hand_over,
        out_shape=(
            jax.ShapeDtypeStruct((owned_rows, win_cols), F32),
            jax.ShapeDtypeStruct((1, owned_rows), F32),
        ),
        in_specs=[vmem],
        out_specs=(vmem, vmem),
        name="hand_over",
    )(pltpu.with_memory_space_constraint(result, pltpu.VMEM))
    return coadd, weight_map.reshape(owned_rows)


def solution(mesh):
    return jax.shard_map(
        on_device,
        mesh=mesh,
        in_specs=(
            P(("groups", "sky"), None, None),
            P(),
            P(),
            P(("groups", "sky"), None, None),
            P(("groups", "sky"), None),
            P(("groups", "sky")),
            P("groups"),
            P(("groups", "sky")),
            P(("groups", "sky")),
        ),
        out_specs=(P(("groups", "sky"), None), P(("groups", "sky"))),
        check_vma=False,
    )
```

```python
import functools

import jax
import jax.numpy as jnp
from jax import lax
from jax.experimental import pallas as pl
from jax.experimental.pallas import tpu as pltpu
from jax.sharding import PartitionSpec as P

TILE_R = 8
BLK_DEV = 16
LANES = 128
STEPS = 4
F32 = jnp.float32
BF16 = jnp.bfloat16


def iota(shape, axis):
    return lax.broadcasted_iota(jnp.int32, shape, axis)


def dot(lhs, rhs):
    return jnp.dot(lhs, rhs, preferred_element_type=F32)


def onehot(mask):
    return jnp.where(mask, 1.0, 0.0).astype(BF16)


def lanczos(fraction):
    lane = iota((1, LANES), 1)
    offsets = (lane - 2).astype(F32) - fraction
    offsets = jnp.where(lane < 6, offsets, 0.5)
    angles = jnp.pi * offsets
    thirds = angles / 3.0
    kernel = jnp.sin(angles) / angles * (jnp.sin(thirds) / thirds)
    kernel = jnp.where(lane < 6, kernel, 0.0)
    return kernel / jnp.sum(kernel, axis=1, keepdims=True)


def kernel(
    sky,
    image_ref,
    row_taps_ref,
    col_taps_ref,
    mix_ref,
    shift_ref,
    visit_ref,
    visit_weight_ref,
    block_ref,
    offset_ref,
    result_ref,
    xpad,
    pick,
    taps2d,
    acc,
    spread_pad,
    meta_send,
    meta_recv,
    data_send,
    data_recv,
    meta_ssem,
    meta_rsem,
    data_ssem,
    data_rsem,
):
    me = lax.axis_index("sky")
    win_rows, win_cols = image_ref.shape
    tap_count, basis = row_taps_ref.shape
    half = tap_count // 2
    tiles = block_ref.shape[1]
    cap = max(2, tiles // sky)
    span = cap * TILE_R
    owned_rows = BLK_DEV * TILE_R
    blk_shift = BLK_DEV.bit_length() - 1

    barrier = pltpu.get_barrier_semaphore()

    def greet(step, carry):
        pl.semaphore_signal(
            barrier,
            inc=1,
            device_id={"sky": lax.rem(me + step, sky)},
            device_id_type=pl.DeviceIdType.MESH,
        )
        return carry

    lax.fori_loop(1, sky, greet, 0)

    block = block_ref[...]
    owner_i = lax.shift_right_logical(block, blk_shift)
    start_row = ((block - owner_i * BLK_DEV) * TILE_R + offset_ref[...]).astype(F32)
    owner_row = owner_i.astype(F32)
    eye = iota((tiles, tiles), 0) == iota((tiles, tiles), 1)
    column = lambda row: jnp.sum(
        jnp.where(eye, jnp.broadcast_to(row, (tiles, tiles)), 0.0), axis=1, keepdims=True
    )
    owner_col = column(owner_row)
    start_col = column(start_row)
    same = owner_col == owner_row
    below = iota((tiles, tiles), 0) < iota((tiles, tiles), 1)
    above = iota((tiles, tiles), 1) < iota((tiles, tiles), 0)
    rank_row = jnp.sum(jnp.where(same & below, 1.0, 0.0), axis=0, keepdims=True)
    rank_col = jnp.sum(jnp.where(same & above, 1.0, 0.0), axis=1, keepdims=True)
    visits = visit_weight_ref.shape[1]
    own_weight = jnp.sum(
        jnp.where(
            iota((1, visits), 1) == visit_ref[...], visit_weight_ref[...].astype(F32), 0.0
        ),
        axis=1,
        keepdims=True,
    )

    per_group = LANES // span
    spill_group = min(LANES // TILE_R, sky)
    sub = iota((sky * TILE_R, tiles), 0)
    owner_of = lax.shift_right_logical(sub, 3).astype(F32)
    lane = iota((tiles, LANES), 1)
    mine = lax.div(lane, jnp.int32(span)) == lax.rem(me, per_group)
    slot_rank = lax.div(lax.rem(lane, jnp.int32(span)), jnp.int32(TILE_R)).astype(F32)
    in_eight = lax.rem(lane, jnp.int32(TILE_R)).astype(F32)
    landing = jnp.where(mine & (slot_rank == rank_col), start_col + in_eight + 1.0, 0.0)
    targets = dot(onehot(owner_of == owner_row), landing.astype(BF16))
    mine = lax.div(lane, jnp.int32(TILE_R)) == lax.rem(me, spill_group)
    cover = onehot(mine & (start_col > in_eight + float(owned_rows - TILE_R)))
    covered = dot(onehot(owner_of - 1.0 == owner_row), cover)
    lane8 = iota((sky * TILE_R, LANES), 1)
    sub8 = lax.rem(iota((sky * TILE_R, LANES), 0), jnp.int32(TILE_R))
    weight8 = jnp.broadcast_to(own_weight, (sky * TILE_R, LANES))
    tile_lanes = lax.div(lane8, jnp.int32(span)) == lax.rem(me, per_group)
    spill_lanes = lax.div(lane8, jnp.int32(TILE_R)) == lax.rem(me, spill_group)
    header = jnp.where((sub8 == 1) & tile_lanes, weight8, 0.0)
    header = jnp.where((sub8 == 2) & spill_lanes, weight8, header)
    header = jnp.where(sub8 == 3, covered, header)
    header = jnp.where(sub8 == 0, targets, header)
    meta_send[...] = header.reshape(sky, TILE_R, LANES).astype(BF16)

    def message(send, recv, ssem, rsem, turn):
        to = lax.rem(me + turn, sky)
        return pltpu.make_async_remote_copy(
            src_ref=send.at[to],
            dst_ref=recv.at[me],
            send_sem=ssem,
            recv_sem=rsem,
            device_id={"sky": to},
            device_id_type=pl.DeviceIdType.MESH,
        )

    def wait_all(send, recv, ssem, rsem):
        copy = pltpu.make_async_remote_copy(
            src_ref=send.at[pl.ds(0, sky - 1)],
            dst_ref=recv.at[pl.ds(0, sky - 1)],
            send_sem=ssem,
            recv_sem=rsem,
            device_id={"sky": lax.rem(me + 1, sky)},
            device_id_type=pl.DeviceIdType.MESH,
        )
        copy.wait_send()
        copy.wait_recv()

    def start_meta(step, carry):
        message(meta_send, meta_recv, meta_ssem, meta_rsem, step).start()
        return carry

    def flip(place):
        tap = iota((tap_count, LANES), 0)
        return onehot(
            iota((tap_count, LANES), 1)
            == lax.rem(half + place - tap + LANES, jnp.int32(LANES))
        )

    def flipped(place):
        return lax.dot_general(
            row_taps_ref[...], flip(place), (((0,), (0,)), ((), ())), preferred_element_type=F32
        )

    def mixed(term, taps):
        return jnp.dot(
            col_taps_ref[...].astype(F32) * mix_ref[term],
            taps,
            preferred_element_type=F32,
            precision=lax.Precision.HIGHEST,
        )

    near, far = flipped(0), flipped(LANES // 2)
    taps2d[...] = jnp.zeros_like(taps2d)
    taps2d[0, 0:tap_count, :] = mixed(0, near) + mixed(2, far)
    taps2d[1, 0:tap_count, :] = mixed(1, near)

    xpad[...] = jnp.zeros_like(xpad)
    xpad[pl.ds(16, win_rows), :] = image_ref[...].astype(F32)

    square = (win_cols, win_cols)
    wrapped = lax.rem(iota(square, 1) + LANES // 2, jnp.int32(LANES))
    band = jnp.abs(iota(square, 0) - iota(square, 1)) <= half
    far_band = jnp.abs(iota(square, 0) - wrapped) <= half
    eight = (TILE_R, LANES)
    signed = lax.rem(iota(eight, 1) + LANES // 2, jnp.int32(LANES)) - LANES // 2
    column_pos = (2.0 * signed.astype(F32) + 1.0) / win_cols - 1.0

    def toeplitz(tap):
        fixed, slope = (
            pltpu.roll(
                jnp.broadcast_to(taps2d[term, tap : tap + 1, :], eight),
                0,
                1,
                stride=1,
                stride_axis=0,
            )
            for term in range(2)
        )
        fixed = fixed + column_pos * slope
        rows = []
        for first in range(0, win_cols, TILE_R):
            value = fixed + (2.0 * first / win_cols) * slope
            rows.append(pltpu.roll(value, first, 1) if first else value)
        value = jnp.concatenate(rows, axis=0)
        return jnp.concatenate(
            [jnp.where(band, value, 0.0), jnp.where(far_band, value, 0.0)], axis=1
        ).astype(BF16)

    wide = tiles * TILE_R
    widen = onehot(
        iota((tiles, wide), 0) == lax.shift_right_logical(iota((tiles, wide), 1), 3)
    )
    in_tile = lax.rem(iota((1, wide), 1), jnp.int32(TILE_R)).astype(F32)
    spread8 = lambda row: dot(jnp.broadcast_to(row, (8, tiles)).astype(BF16), widen)[0:1, :]
    slot_lane = spread8(owner_row * cap + rank_row) * TILE_R + in_tile
    past = spread8(start_row) + in_tile - float(owned_rows)
    spill_lane = jnp.where(past >= 0.0, (spread8(owner_row) + 1.0) * TILE_R + past, -1.0)
    sent = sky * span

    def build(first, last):
        left, right = [], []
        for tap in range(first, last):
            right += [toeplitz(tap), toeplitz(tap + 16)]
            moved = xpad[pl.ds(tap + 16 - half, win_rows + 16), :].astype(BF16)
            left += [moved[0:win_rows], moved[16 : win_rows + 16]]
        return jnp.concatenate(left, axis=1), jnp.concatenate(right, axis=0)

    depth = 16 // STEPS
    ready = build(0, depth)
    for step in range(STEPS):
        if step + 1 < STEPS:
            later = build((step + 1) * depth, (step + 2) * depth)
        else:
            pick[0:sent, :] = onehot(iota((sent, wide), 0).astype(F32) == slot_lane)
            pick[sent:, :] = onehot(
                iota((sky * TILE_R, wide), 0).astype(F32) == spill_lane
            )
        term = dot(*ready)
        ready = later
        acc[...] = term if step == 0 else acc[...] + term


    across = lanczos(shift_ref[0:1, 1:2])
    down = lanczos(shift_ref[0:1, 0:1])
    lane = iota((1, win_cols), 1)
    chunk = min(64, win_rows)
    spread_pad[0:8, :] = jnp.zeros((8, win_cols), F32)
    spread_pad[win_rows + 8 : win_rows + 16, :] = jnp.zeros((8, win_cols), F32)
    across_taps = [
        jnp.where((lane + m >= 0) & (lane + m < win_cols), across[0:1, m + 2 : m + 3], 0.0)
        for m in range(-2, 4)
    ]
    down_taps = [
        jnp.broadcast_to(down[0:1, m + 2 : m + 3], (1, win_cols)) for m in range(-2, 4)
    ]
    for first in range(0, win_rows, chunk):
        here = slice(first, first + chunk)
        row_pos = (iota((chunk, win_cols), 0) + first).astype(F32)
        row_pos = (2.0 * row_pos + 1.0) / win_rows - 1.0
        sloped = pltpu.roll(acc[here, win_cols:], LANES // 2, 1)
        matched = acc[here, 0:win_cols] + row_pos * sloped
        spread = across_taps[2] * matched
        for m in (-2, -1, 1, 2, 3):
            spread = spread + across_taps[m + 2] * pltpu.roll(matched, (-m) % win_cols, 1)
        spread_pad[first + 8 : first + 8 + chunk, :] = spread
    warped = []
    for first in range(0, win_rows, chunk):
        value = down_taps[0] * spread_pad[pl.ds(first + 6, chunk), :]
        for m in range(-1, 4):
            value = value + down_taps[m + 2] * spread_pad[pl.ds(first + 8 + m, chunk), :]
        warped.append(value.astype(BF16))
    warped = jnp.concatenate(warped, axis=0)

    packed = dot(pick[...], warped)
    data_send[:, 0:span, :] = packed[0:sent].astype(BF16).reshape(sky, span, win_cols)
    data_send[:, span:, :] = packed[sent:].reshape(sky, TILE_R, win_cols).astype(BF16)

    def start_data(step, carry):
        message(data_send, data_recv, data_ssem, data_rsem, step).start()
        return carry

    pl.semaphore_wait(barrier, sky - 1)
    lax.fori_loop(1, sky, start_meta, 0)
    lax.fori_loop(1, sky, start_data, 0)
    meta_recv[pl.ds(me, 1)] = meta_send[pl.ds(me, 1)]
    data_recv[pl.ds(me, 1)] = data_send[pl.ds(me, 1)]

    wait_all(meta_send, meta_recv, meta_ssem, meta_rsem)

    owned = (owned_rows, LANES)
    row_id = (iota(owned, 0) + 1).astype(F32)
    places = []
    total = jnp.zeros((owned_rows, win_cols), F32)
    ones = jnp.ones((LANES, win_cols), BF16)
    for group in range(sky // per_group):
        head = meta_recv[group * per_group : (group + 1) * per_group]
        head = jnp.sum(head.astype(F32), axis=0)
        place = jnp.where(head[0:1, :] == row_id, head[1:2, :], 0.0).astype(BF16)
        places.append(place)
        total = total + dot(place, ones)
    spill_places = []
    same_row = lax.rem(iota(owned, 1), jnp.int32(TILE_R)) == iota(owned, 0)
    here_row = lax.rem(iota(eight, 1), jnp.int32(TILE_R)) == iota(eight, 0)
    first_rows = jnp.zeros(eight, F32)
    for group in range(sky // spill_group):
        head = meta_recv[group * spill_group : (group + 1) * spill_group]
        head = jnp.sum(head.astype(F32), axis=0)
        spill_places.append(jnp.where(same_row, head[2:3, :], 0.0).astype(BF16))
        count = jnp.sum(jnp.where(here_row, head[2:3, :] * head[3:4, :], 0.0), axis=1, keepdims=True)
        first_rows = first_rows + jnp.broadcast_to(count, eight)
    total = total + jnp.concatenate(
        [first_rows, jnp.zeros((owned_rows - TILE_R, LANES), F32)], axis=0
    )
    diagonal = iota(owned, 0) == iota(owned, 1)
    result_ref[owned_rows:, :] = jnp.broadcast_to(
        jnp.sum(jnp.where(diagonal, total, 0.0), axis=0, keepdims=True), (8, LANES)
    )

    wait_all(data_send, data_recv, data_ssem, data_rsem)
    sums = jnp.zeros((owned_rows, win_cols), F32)
    for group, place in enumerate(places):
        part = data_recv[group * per_group : (group + 1) * per_group, 0:span, :]
        sums = sums + dot(place, part.reshape(LANES, win_cols))
    for group, place in enumerate(spill_places):
        part = data_recv[group * spill_group : (group + 1) * spill_group, span:, :]
        part = part.astype(F32).reshape(spill_group * TILE_R, win_cols).astype(BF16)
        sums = sums + dot(place[:, 0 : spill_group * TILE_R], part)
    result_ref[0:owned_rows, :] = sums / jnp.maximum(total, 1.0)


def hand_over(result_ref, coadd_ref, weight_ref):
    owned_rows = coadd_ref.shape[0]
    coadd_ref[...] = result_ref[0:owned_rows, :]
    weight_ref[...] = result_ref[owned_rows : owned_rows + 1, :]


def on_device(
    image,
    row_taps,
    col_taps,
    mix_coeff,
    shift_frac,
    ccd_visit,
    visit_weight,
    tile_block,
    tile_offset,
):
    sky = lax.axis_size("sky")
    win_rows, win_cols = image.shape[1:]
    tiles = tile_block.shape[0]
    span = max(2, tiles // sky) * TILE_R
    owned_rows = BLK_DEV * TILE_R
    vmem = pl.BlockSpec(memory_space=pltpu.VMEM)
    result = pl.pallas_call(
        functools.partial(kernel, sky),
        out_shape=pltpu.VMEM((owned_rows + 8, win_cols), F32),
        in_specs=[vmem] * 9,
        out_specs=vmem,
        scratch_shapes=[
            pltpu.VMEM((win_rows + 32, win_cols), F32),
            pltpu.VMEM((sky * (span + TILE_R), tiles * TILE_R), BF16),
            pltpu.VMEM((2, 32, LANES), F32),
            pltpu.VMEM((win_rows, 2 * win_cols), F32),
            pltpu.VMEM((win_rows + 16, win_cols), F32),
            pltpu.VMEM((sky, TILE_R, LANES), BF16),
            pltpu.VMEM((sky, TILE_R, LANES), BF16),
            pltpu.VMEM((sky, span + TILE_R, win_cols), BF16),
            pltpu.VMEM((sky, span + TILE_R, win_cols), BF16),
            pltpu.SemaphoreType.DMA,
            pltpu.SemaphoreType.DMA,
            pltpu.SemaphoreType.DMA,
            pltpu.SemaphoreType.DMA,
        ],
        compiler_params=pltpu.CompilerParams(collective_id=0, has_side_effects=True),
        name="coadd",
    )(
        image[0],
        row_taps.T,
        col_taps.T,
        mix_coeff.transpose(1, 0, 2),
        shift_frac,
        ccd_visit.reshape(1, 1),
        visit_weight.reshape(1, -1),
        tile_block.reshape(1, -1),
        tile_offset.reshape(1, -1),
    )
    coadd, weight_map = pl.pallas_call(
        hand_over,
        out_shape=(
            jax.ShapeDtypeStruct((owned_rows, win_cols), F32),
            jax.ShapeDtypeStruct((1, owned_rows), F32),
        ),
        in_specs=[vmem],
        out_specs=(vmem, vmem),
        name="hand_over",
    )(pltpu.with_memory_space_constraint(result, pltpu.VMEM))
    return coadd, weight_map.reshape(owned_rows)


def solution(mesh):
    return jax.shard_map(
        on_device,
        mesh=mesh,
        in_specs=(
            P(("groups", "sky"), None, None),
            P(),
            P(),
            P(("groups", "sky"), None, None),
            P(("groups", "sky"), None),
            P(("groups", "sky")),
            P("groups"),
            P(("groups", "sky")),
            P(("groups", "sky")),
        ),
        out_specs=(P(("groups", "sky"), None), P(("groups", "sky"))),
        check_vma=False,
    )
```
